512 devices in a mesh: lon: 128 (over x_lo, z, y), lat: 4 (over x_hi, core).
Axes of the slice: x: 4 (x_hi: 2, x_lo: 2; x = x_hi * 2 + x_lo), y: 4, z: 16, core: 2. Of those that a mesh axis runs over, the one named last changes fastest.
Arguments:
- queries: bfloat16 [64, 2048, 256], P('lat', 'lon'), may hold values from -11 to 11
- key_values: bfloat16 [2, 64, 2048, 256], P(None, 'lat', 'lon'), may hold values from -11 to 11
- pole_mask: int32 [8], replicated, may hold values 0 or 1
- sea_mask: int32 [8, 256], replicated, may hold values 0 or 1
- reg_queries: bfloat16 [256, 256], replicated, may hold values from -21 to 21
- reg_keys: bfloat16 [256, 256], replicated, may hold values from -6 to 6
Outputs:
- attended: bfloat16 [64, 2048, 256], P('lat', 'lon')
- reg_out: bfloat16 [256, 256], replicated
The draws below stay inside these ranges and needn't reach their ends.
All inputs are finite; a program needn't handle non-finite values.
Results may differ from the reference program's by a relative error of at most 0.0048.
Values may be sent and summed in bfloat16 or wider, within the bound.
A program may use at most 64 MiB of HBM per device.

```python
import jax
import jax.numpy as jnp
from jax import lax

HEADS = 4
HEAD_DIM = 64
NREG = 256
RADIUS = 6
TILE = 8
QROWS = 16
CHANNELS = 256
NLAT = 64
NLON = 2048


def shared_keys(key):
    base = jax.random.fold_in(key, 7)
    first = jax.random.fold_in(base, 0)
    return jnp.clip(jax.random.normal(first, (NLAT, NLON, HEADS * HEAD_DIM), jnp.float32), -6.0, 6.0)


def draw_key_values(key, part):
    channels = HEADS * HEAD_DIM
    keys_drawn = shared_keys(key)
    value_key = jax.random.fold_in(key, 9)
    values_drawn = jnp.clip(jax.random.normal(value_key, (NLAT, NLON, channels), jnp.float32), -6.0, 6.0)
    return jnp.stack([keys_drawn, values_drawn]).astype(jnp.bfloat16)


def draw_queries(key, part):
    channels = HEADS * HEAD_DIM
    noise_key = jax.random.fold_in(key, 13)
    drawn = jnp.clip(jax.random.normal(noise_key, (NLAT, NLON, channels), jnp.float32), -6.0, 6.0)
    return drawn.astype(jnp.bfloat16)


def draw_reg_queries(key, part):
    channels = HEADS * HEAD_DIM
    noise_key = jax.random.fold_in(key, 17)
    drawn = 3.5 * jnp.clip(jax.random.normal(noise_key, (NREG, channels), jnp.float32), -6.0, 6.0)
    return drawn.astype(jnp.bfloat16)


def touch_ends(result, own_key, low, high):
    longest = result.shape.index(max(result.shape))
    spots = []
    for shift in (0, 1):
        where = [jax.random.randint(jax.random.fold_in(own_key, axis), (), 0, length) for axis, length in enumerate(result.shape)]
        where[longest] = (where[longest] + shift) % result.shape[longest]
        spots.append(tuple(where))
    return result.at[spots[0]].set(low).at[spots[1]].set(high)


def bell_draw(stream_key, extent, deviation, bound, kind=jnp.bfloat16):
    return jnp.clip(deviation * jax.random.normal(stream_key, extent, jnp.float32), -bound, bound).astype(kind)


def setup_inputs(seed: int = 0) -> dict:
    key_list = jax.random.split(jax.random.key(seed), 7)
    queries = draw_queries(jax.random.fold_in(key_list[6], 71), 0)
    key_values = draw_key_values(jax.random.fold_in(key_list[6], 71), 0)
    pole_mask = touch_ends((jax.random.randint(key_list[2], (NLAT // TILE,), 0, 4) < 3).astype(jnp.int32), jax.random.fold_in(key_list[2], 1), 0, 1)
    sea_mask = touch_ends((jax.random.randint(key_list[3], (NLAT // TILE, NLON // TILE), 0, 3) < 2).astype(jnp.int32), jax.random.fold_in(key_list[3], 1), 0, 1)
    reg_queries = draw_reg_queries(jax.random.fold_in(key_list[6], 71), 0)
    reg_keys = bell_draw(key_list[5], (NREG, CHANNELS), 1.0, 6.0)
    return {"queries": queries, "key_values": key_values, "pole_mask": pole_mask, "sea_mask": sea_mask, "reg_queries": reg_queries, "reg_keys": reg_keys}


def cell_keep(pole_mask, sea_mask):
    tiles = pole_mask[:, None] * sea_mask
    return jnp.repeat(jnp.repeat(tiles, TILE, axis=0), TILE, axis=1)


def register_pass(reg_queries, key_values):
    scale_factor = HEAD_DIM ** -0.5
    heads_query = reg_queries.astype(jnp.float32).reshape(NREG, HEADS, HEAD_DIM)
    block_count = NLAT // QROWS
    block_keys = key_values[0].reshape(block_count, QROWS * NLON, HEADS, HEAD_DIM)
    block_values = key_values[1].reshape(block_count, QROWS * NLON, HEADS, HEAD_DIM)

    def block_scores(keys_block):
        return jnp.einsum("rhd,khd->hrk", heads_query, keys_block.astype(jnp.float32)) * scale_factor

    def step_max(running, keys_block):
        return jnp.maximum(running, jnp.max(block_scores(keys_block), axis=2)), None

    highest, unused = lax.scan(step_max, jnp.full((HEADS, NREG), -jnp.inf, jnp.float32), block_keys)

    def step_sum(running, block_pair):
        weights = jnp.exp(block_scores(block_pair[0]) - highest[:, :, None])
        rounded = lax.optimization_barrier(weights.astype(jnp.bfloat16)).astype(jnp.float32)
        added = jnp.einsum("hrk,khd->rhd", rounded, block_pair[1].astype(jnp.float32))
        return (running[0] + jnp.sum(weights, axis=2), running[1] + added), None

    initial = (jnp.zeros((HEADS, NREG), jnp.float32), jnp.zeros((NREG, HEADS, HEAD_DIM), jnp.float32))
    (weight_sums, weighted), unused = lax.scan(step_sum, initial, (block_keys, block_values))
    return (weighted / weight_sums.T[:, :, None]).astype(jnp.bfloat16).reshape(NREG, HEADS * HEAD_DIM)


def reference(queries, key_values, pole_mask, sea_mask, reg_queries, reg_keys):
    scale_factor = HEAD_DIM ** -0.5
    channels = HEADS * HEAD_DIM
    span = 2 * RADIUS + 1
    reg_values = register_pass(reg_queries, key_values)
    keep = cell_keep(pole_mask, sea_mask)
    padded = jnp.pad(key_values, ((0, 0), (RADIUS, RADIUS), (0, 0), (0, 0)))
    padded = jnp.concatenate([padded[:, :, NLON - RADIUS:], padded, padded[:, :, :RADIUS]], axis=2)
    keep_pad = jnp.pad(keep, ((RADIUS, RADIUS), (0, 0)))
    keep_pad = jnp.concatenate([keep_pad[:, NLON - RADIUS:], keep_pad, keep_pad[:, :RADIUS]], axis=1)
    reg_key_heads = reg_keys.astype(jnp.float32).reshape(NREG, HEADS, HEAD_DIM)
    reg_value_heads = reg_values.astype(jnp.float32).reshape(NREG, HEADS, HEAD_DIM)
    offsets = jnp.arange(span * span, dtype=jnp.int32)

    def one_block(first_row):
        block_queries = lax.dynamic_slice_in_dim(queries, first_row, QROWS, 0).astype(jnp.float32)
        block_queries = block_queries.reshape(QROWS, NLON, HEADS, HEAD_DIM)

        def shifted(offset):
            lat_shift = offset // span
            lon_shift = offset % span
            zero_index = jnp.zeros((), jnp.int32)
            window = lax.dynamic_slice(padded, (zero_index, first_row + lat_shift, lon_shift, zero_index), (2, QROWS, NLON, channels))
            mask_window = lax.dynamic_slice(keep_pad, (first_row + lat_shift, lon_shift), (QROWS, NLON))
            return window, mask_window

        def near_score(offset):
            window, mask_window = shifted(offset)
            keys_here = window[0].astype(jnp.float32).reshape(QROWS, NLON, HEADS, HEAD_DIM)
            scores = jnp.sum(block_queries * keys_here, axis=3) * scale_factor
            return jnp.where(mask_window[:, :, None] > 0, scores, -jnp.inf)

        near_scores = lax.map(near_score, offsets)
        reg_scores = jnp.einsum("ijhd,rhd->ijhr", block_queries, reg_key_heads) * scale_factor
        highest = jnp.maximum(jnp.max(near_scores, axis=0), jnp.max(reg_scores, axis=3))
        near_weights = jnp.exp(near_scores - highest[None])
        reg_weights = jnp.exp(reg_scores - highest[:, :, :, None])
        weight_sums = jnp.sum(near_weights, axis=0) + jnp.sum(reg_weights, axis=3)
        near_rounded = lax.optimization_barrier(near_weights.astype(jnp.bfloat16)).astype(jnp.float32)
        reg_rounded = lax.optimization_barrier(reg_weights.astype(jnp.bfloat16)).astype(jnp.float32)

        def add_offset(running, offset):
            window, unused_mask = shifted(offset)
            values_here = window[1].astype(jnp.float32).reshape(QROWS, NLON, HEADS, HEAD_DIM)
            weight_here = lax.dynamic_index_in_dim(near_rounded, offset, 0, keepdims=False)
            return running + weight_here[..., None] * values_here, None

        start_value = jnp.einsum("ijhr,rhd->ijhd", reg_rounded, reg_value_heads)
        mixture, unused = lax.scan(add_offset, start_value, offsets)
        return (mixture / weight_sums[..., None]).astype(jnp.bfloat16).reshape(QROWS, NLON, channels)

    starts = jnp.arange(NLAT // QROWS, dtype=jnp.int32) * QROWS
    attended = lax.map(one_block, starts).reshape(NLAT, NLON, channels)
    return (attended, reg_values)
```

```python
import functools

import jax
import jax.numpy as jnp
from jax import lax
from jax.experimental import pallas as pl
from jax.experimental.pallas import tpu as pltpu
from jax.sharding import PartitionSpec as P

HEADS = 4
HEAD_DIM = 64
NREG = 256
RADIUS = 6
TILE = 8
CHANNELS = 256
ROWS = 16
COLS = 16
CELLS = ROWS * COLS
SIDE = ROWS * TILE
KEYS = 896
LOG2_SCALE = HEAD_DIM ** (-0.5) * 1.4426950408889634
NX, NY, NZ = 4, 4, 16
OWN = 8
WIDE = CHANNELS + 128
MASKED = -1e30
MESH = pl.DeviceIdType.MESH

PLANE = sorted(
    [(c, x, y) for c in range(2) for x in range(NX) for y in range(NY) if (c, x, y) != (0, 0, 0)],
    key=lambda o: -(min(o[1], NX - o[1]) + min(o[2], NY - o[2])),
)
LINE = sorted(range(1, NZ), key=lambda k: -min(k, NZ - k))

PIECES = (
    (256, 128, 0, 1),
    (384, 128, 0, -1),
    (512, 96, -1, 0),
    (608, 96, 1, 0),
    (704, 48, -1, -1),
    (752, 48, -1, 1),
    (800, 48, 1, -1),
    (848, 48, 1, 1),
)


def place():
    lon, lat = lax.axis_index("lon"), lax.axis_index("lat")
    return lat % 2, (lat // 2) * 2 + lon // (NY * NZ), lon % NY, (lon // NY) % NZ


def device(core, x, y, z):
    return {"lon": (x % 2) * (NY * NZ) + z * NY + y, "lat": (x // 2) * 2 + core}


def nt(a, b):
    return lax.dot_general(a, b, (((1,), (1,)), ((), ())), preferred_element_type=jnp.float32)


def nn(a, b):
    return jnp.dot(a, b, preferred_element_type=jnp.float32)


def head_of(rows, lanes=CHANNELS):
    return lax.broadcasted_iota(jnp.int32, (rows, lanes), 1) // HEAD_DIM


def only(head, lanes, x):
    return jnp.where(lanes == head, x.astype(jnp.float32), 0.0).astype(jnp.bfloat16)


def merge(theirs, mine):
    logs, own_log = theirs[:, :, CHANNELS:], mine[:, CHANNELS:]
    top = jnp.maximum(jnp.max(logs, axis=0), own_log)
    part = jnp.exp2(logs - top[None])
    own_part = jnp.exp2(own_log - top)
    total = jnp.sum(part, axis=0) + own_part
    low = lax.broadcasted_iota(jnp.int32, (OWN, 128), 1) < HEAD_DIM

    def spread(x, half):
        return jnp.where(low, x[..., 2 * half : 2 * half + 1], x[..., 2 * half + 1 : 2 * half + 2])

    out = []
    for half in range(2):
        cols = slice(128 * half, 128 * half + 128)
        summed = spread(own_part, half) * mine[:, cols]
        summed = summed + jnp.sum(spread(part, half) * theirs[:, :, cols], axis=0)
        out.append(summed / spread(total, half))
    return out, top + jnp.log2(total)


def kernel(
    pole, sea, q, kv, rq, rk, att, reg_out,
    window, sides, msg1, buf1, msg2, buf2, final, reg_w, near, inverse, bias,
    hs, hr, s1, r1, s2, r2, s3, r3,
):
    core, x, y, z = place()
    lon, lat = lax.axis_index("lon"), lax.axis_index("lat")
    lons, lats = lax.axis_size("lon"), lax.axis_size("lat")
    me = (core * NX + x) * NY + y
    plane = [(lax.rem(core + c, 2), lax.rem(x + a, NX), lax.rem(y + b, NY)) for c, a, b in PLANE]
    plane_ids = [device(c, a, b, z) for c, a, b in plane]
    line_ids = [device(core, x, y, lax.rem(z + k, NZ)) for k in LINE]
    halo_ids = [
        {"lon": lax.rem(lon - b + lons, lons), "lat": lax.rem(lat - a + lats, lats)}
        for _, _, a, b in PIECES
    ]
    barrier = pltpu.get_barrier_semaphore()
    for other in plane_ids + line_ids + halo_ids:
        pl.semaphore_signal(barrier, inc=1, device_id=other, device_id_type=MESH)

    lanes = head_of(NREG)
    stat_lane = lax.broadcasted_iota(jnp.int32, (NREG, 128), 1)
    keys, values = kv[0], kv[1]
    gathered = jnp.zeros((NREG, CHANNELS), jnp.float32)
    logs = jnp.zeros((NREG, 128), jnp.float32)
    for h in range(HEADS):
        scores = nt(only(h, lanes, rq[...]), keys) * LOG2_SCALE
        top = jnp.max(scores, axis=1, keepdims=True)
        weights = jnp.exp2(scores - top)
        total = jnp.sum(weights, axis=1, keepdims=True)
        mixed = nn(weights.astype(jnp.bfloat16), values) / total
        gathered = jnp.where(lanes == h, mixed, gathered)
        logs = jnp.where(stat_lane == h, top + jnp.log2(total), logs)
    msg1[:, :, :CHANNELS] = gathered.reshape(NREG // OWN, OWN, CHANNELS)
    msg1[:, :, CHANNELS:] = logs.reshape(NREG // OWN, OWN, 128)

    for i in range(2):
        window[i, :CELLS] = kv[i]
        split = kv[i].astype(jnp.float32).reshape(ROWS, 2, TILE, CHANNELS)
        for side in range(2):
            sides[side, i] = split[:, side].reshape(SIDE, CHANNELS).astype(jnp.bfloat16)

    pl.semaphore_wait(barrier, len(plane_ids) + len(line_ids) + len(halo_ids))
    for k, (c, a, b) in enumerate(plane):
        pltpu.make_async_remote_copy(
            msg1.at[(c * NX + a) * NY + b], buf1.at[k], s1, r1, device_id=plane_ids[k], device_id_type=MESH
        ).start()
    for k, (first, count, a, b) in enumerate(PIECES):
        if b == 0:
            own = pl.ds(0 if a > 0 else CELLS - count, count)
            source = window.at[:, own]
        else:
            own = pl.ds(0 if a >= 0 else SIDE - count, count)
            source = sides.at[0 if b > 0 else 1, :, own]
        pltpu.make_async_remote_copy(
            source, window.at[:, pl.ds(first, count)], hs, hr, device_id=halo_ids[k], device_id_type=MESH
        ).start()

    spot = lax.broadcasted_iota(jnp.int32, (1, KEYS), 1)
    key_lat = jnp.zeros((1, KEYS), jnp.int32)
    key_lon = jnp.zeros((1, KEYS), jnp.int32)
    for first, count, a, b in ((0, CELLS, 0, 0),) + PIECES:
        width = COLS if b == 0 else TILE
        here = (spot >= first) & (spot < first + count)
        base_lat = 0 if a == 0 else (-RADIUS if a < 0 else ROWS)
        base_lon = 0 if b == 0 else (-TILE if b < 0 else COLS)
        key_lat = jnp.where(here, base_lat + (spot - first) // width, key_lat)
        key_lon = jnp.where(here, base_lon + (spot - first) % width, key_lon)
    tile_lat, tile_lon = (key_lat + TILE) // TILE, (key_lon + TILE) // TILE
    kept = jnp.zeros((1, KEYS), jnp.int32)
    tile_rows, tile_cols = 8, 256
    for a in range(4):
        row = lat * 2 - 1 + a
        inside = jnp.where((row >= 0) & (row < tile_rows), 1, 0)
        row = jnp.clip(row, 0, tile_rows - 1)
        band = pole[row] * inside
        for b in range(4):
            col = lax.rem(lon * 2 - 1 + b + tile_cols, tile_cols)
            kept = jnp.where((tile_lat == a) & (tile_lon == b), band * sea[row, col], kept)
    cell = lax.broadcasted_iota(jnp.int32, (CELLS, 1), 0)
    near_by = (
        (jnp.abs(key_lat - cell // COLS) <= RADIUS)
        & (jnp.abs(key_lon - cell % COLS) <= RADIUS)
        & (kept > 0)
    )
    bias[...] = jnp.where(near_by, 0.0, MASKED)

    pltpu.make_async_copy(buf1, buf1, r1).wait()
    halves, log = merge(buf1[...], msg1[me])
    for half in range(2):
        msg2[:, 128 * half : 128 * half + 128] = halves[half]
    msg2[:, CHANNELS:] = log
    for k, other in enumerate(line_ids):
        pltpu.make_async_remote_copy(
            msg2, buf2.at[k], s2, r2, device_id=other, device_id_type=MESH
        ).start()

    pltpu.make_async_copy(window.at[:, pl.ds(CELLS, KEYS - CELLS)], window.at[:, pl.ds(CELLS, KEYS - CELLS)], hr).wait()
    mixture = jnp.zeros((CELLS, CHANNELS), jnp.float32)
    totals = jnp.zeros((CELLS, CHANNELS), jnp.float32)
    for h in range(HEADS):
        query = only(h, lanes, q[...])
        near_scores = nt(query, window[0]) * LOG2_SCALE + bias[...]
        reg_scores = nt(query, rk[...]) * LOG2_SCALE
        top = jnp.maximum(
            jnp.max(near_scores, axis=1, keepdims=True), jnp.max(reg_scores, axis=1, keepdims=True)
        )
        near_weights = jnp.exp2(near_scores - top)
        reg_weights = jnp.exp2(reg_scores - top)
        total = jnp.sum(near_weights, axis=1, keepdims=True) + jnp.sum(reg_weights, axis=1, keepdims=True)
        reg_w[h] = reg_weights.astype(jnp.bfloat16)
        mixture = jnp.where(lanes == h, nn(near_weights.astype(jnp.bfloat16), window[1]), mixture)
        totals = jnp.where(lanes == h, total, totals)
    near[...] = mixture
    inverse[...] = 1.0 / totals

    pltpu.make_async_copy(buf2, buf2, r2).wait()
    halves, _ = merge(buf2[...], msg2[...])
    for half in range(2):
        final[me, :, 128 * half : 128 * half + 128] = halves[half].astype(jnp.bfloat16)
    for k, other in enumerate(plane_ids):
        pltpu.make_async_remote_copy(
            final.at[me], final.at[me], s3, r3, device_id=other, device_id_type=MESH
        ).start()

    pltpu.make_async_copy(final.at[pl.ds(0, 31)], final.at[pl.ds(0, 31)], r3).wait()
    reg_values = final[...].astype(jnp.float32).reshape(NREG, CHANNELS).astype(jnp.bfloat16)
    reg_out[...] = reg_values
    mixture = jnp.zeros((CELLS, CHANNELS), jnp.float32)
    for h in range(HEADS):
        mixture = jnp.where(lanes == h, nn(reg_w[h], reg_values), mixture)
    att[...] = ((near[...] + mixture) * inverse[...]).astype(jnp.bfloat16)

    pltpu.make_async_copy(buf1, buf1, s1).wait()
    pltpu.make_async_copy(window.at[:, pl.ds(CELLS, KEYS - CELLS)], window.at[:, pl.ds(CELLS, KEYS - CELLS)], hs).wait()
    pltpu.make_async_copy(buf2, buf2, s2).wait()
    pltpu.make_async_copy(final.at[pl.ds(0, 31)], final.at[pl.ds(0, 31)], s3).wait()


def shards(queries, key_values, pole_mask, sea_mask, reg_queries, reg_keys):
    vmem = pl.BlockSpec(memory_space=pltpu.VMEM)
    smem = pl.BlockSpec(memory_space=pltpu.SMEM)
    att, reg_vals = pl.pallas_call(
        kernel,
        out_shape=(
            jax.ShapeDtypeStruct((CELLS, CHANNELS), jnp.bfloat16),
            jax.ShapeDtypeStruct((NREG, CHANNELS), jnp.bfloat16),
        ),
        in_specs=[smem, smem, vmem, vmem, vmem, vmem],
        out_specs=(vmem, vmem),
        scratch_shapes=[
            pltpu.VMEM((2, KEYS, CHANNELS), jnp.bfloat16),
            pltpu.VMEM((2, 2, SIDE, CHANNELS), jnp.bfloat16),
            pltpu.VMEM((32, OWN, WIDE), jnp.float32),
            pltpu.VMEM((31, OWN, WIDE), jnp.float32),
            pltpu.VMEM((OWN, WIDE), jnp.float32),
            pltpu.VMEM((NZ - 1, OWN, WIDE), jnp.float32),
            pltpu.VMEM((32, OWN, CHANNELS), jnp.bfloat16),
            pltpu.VMEM((HEADS, CELLS, NREG), jnp.bfloat16),
            pltpu.VMEM((CELLS, CHANNELS), jnp.float32),
            pltpu.VMEM((CELLS, CHANNELS), jnp.float32),
            pltpu.VMEM((CELLS, KEYS), jnp.float32),
        ]
        + [pltpu.SemaphoreType.DMA] * 8,
        compiler_params=pltpu.CompilerParams(
            collective_id=0, has_side_effects=True, vmem_limit_bytes=48 * 2**20
        ),
    )(
        pole_mask,
        sea_mask,
        queries.reshape(CELLS, CHANNELS),
        key_values.reshape(2, CELLS, CHANNELS),
        reg_queries,
        reg_keys,
    )
    return att.reshape(queries.shape), reg_vals


def solution(mesh):
    return jax.shard_map(
        shards,
        mesh=mesh,
        in_specs=(P("lat", "lon", None), P(None, "lat", "lon", None), P(), P(), P(), P()),
        out_specs=(P("lat", "lon", None), P()),
        check_vma=False,
    )
```
